32 devices in a mesh: groups: 2 (over y), expert: 4 (over z), tensor: 4 (over x, core).
Axes of the slice: x: 2, y: 2, z: 4, core: 2. Of those that a mesh axis runs over, the one named last changes fastest.
Arguments:
- tokens: bfloat16 [1024, 4096], P(('groups', 'expert'), 'tensor'), parts along dimension 0, may hold values from -130 to 130
- norm_gain: float32 [4096], replicated, may hold values from 0.5 to 1.5
- router: bfloat16 [4096, 8], replicated, may hold values from -0.09375 to 0.09375
- expert_ids: int32 [1024, 2], P(('groups', 'expert')), parts along dimension 0, may hold values from 0 to 7, all different within a row; in each aligned block of 128 rows (0 to 127, 128 to 255, ...) at most 40 rows name the same one
- w_gate: bfloat16 [4, 2, 4096, 7168], P('expert', None, None, 'tensor'), may hold values from -0.09375 to 0.09375
- w_down: bfloat16 [4, 2, 7168, 4096], P('expert', None, None, 'tensor'), may hold values from -0.0625 to 0.0625
Outputs:
- mixed: bfloat16 [1024, 4096], P(('groups', 'expert'), 'tensor'), parts along dimension 0
The draws below stay inside these ranges and needn't reach their ends.
There are 2 independent parts, one for each index of `groups`. The reference program is written for one: setup_inputs(seed, part) draws one part's arguments, and reference() takes and returns one part's arrays. A program takes and returns all parts, laid end to end along the dimension named above; an argument that names none is the same for every part. Nothing has to cross between parts.
Inputs may be any that keep to these rules, and one draw needn't show every extreme that they name: `expert_ids`: each row names two different experts; within each aligned block of 128 rows (the tokens of one index of the expert axis) no expert is named by more than 40 rows, a bound that some block reaches.
All inputs are finite; a program needn't handle non-finite values.
Results may differ from the reference program's by a relative error of at most 0.0085.
Values may be sent and summed in bfloat16 or wider, within the bound.
A program may use at most 128 MiB of HBM per device.

```python
import math
from functools import partial
import jax
import jax.numpy as jnp
import numpy as np
from jax import lax

D = 4096
EXPERTS = 8
FF = 7168
TOK_DEV = 128
CAP = 40
PIECES = 1
LOCAL = 2
FF_IDX = 7168
TOKENS = 512
N_EXPERT = 4


def draw_tokens(key, part):
    keys = jax.random.split(key, 3)
    row_scale = jnp.exp(jax.random.uniform(keys[0], (TOKENS, 1), jnp.float32, math.log(0.3), math.log(3.0)))
    position = jnp.arange(D, dtype=jnp.float32) / (D - 1)
    rough = jnp.exp(jax.random.uniform(keys[1], (1, D), jnp.float32, -0.3, 0.3))
    column_scale = 0.5 * jnp.exp(position * math.log(10.0))[None, :] * rough
    base = jax.random.normal(keys[2], (TOKENS, D), jnp.float32)
    return (jnp.clip(base, -6.0, 6.0) * row_scale * column_scale).astype(jnp.bfloat16)


def block_scale(key, shape, cuts, smallest, largest):
    def one(dim, parts):
        draws = jax.random.uniform(jax.random.fold_in(jax.random.fold_in(key, 6), dim), (parts,), jnp.float32, smallest / len(cuts), largest / len(cuts))
        return jnp.repeat(jnp.exp(draws), shape[dim] // parts).reshape((-1,) + (1,) * (len(shape) - dim - 1))

    loudness = one(*cuts[0])
    for cut in cuts[1:]:
        loudness = loudness * one(*cut)
    return loudness


def deal_out(rng, own, number, rows, amount, top, reach, skew):
    ranking = jax.random.permutation(rng, amount)
    heavy_load, usual = shares(amount, rows * top, reach, skew, True), shares(amount, rows * top, reach, skew, False)
    places = jnp.arange(amount)

    def named(lengths, turn):
        used = int((lengths > 0).sum())
        fixed = max(1, used // 4)
        shifted = fixed + (places - fixed + turn * (used - fixed)) % max(1, amount - fixed)
        return jnp.zeros((amount,), jnp.int32).at[ranking[jnp.where(places < fixed, places, shifted)]].set(jnp.asarray(lengths, jnp.int32))

    lengths = jnp.where(number % 4 == 0, named(heavy_load, number // 4), named(usual, number - number // 4 - 1))
    mixed = jax.random.permutation(jax.random.fold_in(own, 3), amount)
    source_of, sink = mixed[0:amount // 2 * 2:2], mixed[1:amount // 2 * 2:2]
    margin = jnp.minimum(lengths[source_of] - 1, reach - lengths[sink]) // 2
    margin = jnp.where((source_of == ranking[0]) | (sink == ranking[0]) | (lengths[sink] == 0), 0, jnp.maximum(margin, 0))
    shifted = jax.random.randint(jax.random.fold_in(own, 4), (amount // 2,), 0, 1 << 20) % (margin + 1)
    lengths = lengths.at[source_of].add(-shifted).at[sink].add(shifted)
    items = jnp.searchsorted(jnp.cumsum(lengths), jnp.arange(rows * top), side="right").astype(jnp.int32)
    listing = items.reshape(top, rows).T
    listing = listing[jax.random.permutation(jax.random.fold_in(own, 1), rows)]
    turn = jax.random.randint(jax.random.fold_in(own, 2), (rows, 1), 0, top)
    return jnp.take_along_axis(listing, (jnp.arange(top)[None, :] + turn) % top, axis=1)


def shares(amount, total, bound, slope, full):
    weights = [(1 << 20) // math.isqrt(standing ** slope) + 1 for standing in range(1, amount + 1)]
    largest = bound if full else min(bound, max(-(-total // amount), total * weights[0] // sum(weights)))
    least = 1 if total - largest >= amount - 1 else 0
    holding, surplus = [largest] + [least] * (amount - 1), total - largest - least * (amount - 1)
    while surplus > 0:
        movable = [i for i in range(1, amount) if holding[i] < largest] or [i for i in range(1, amount) if holding[i] < bound]
        mass, left = sum([weights[i] for i in movable]), surplus
        for i in movable:
            more = min(bound - holding[i], max(1, left * weights[i] // mass), surplus)
            holding[i] = holding[i] + more
            surplus = surplus - more
    return np.array(holding)


def noise(own_key, extent, scale, reach, cuts=(), kind=jnp.bfloat16):
    array = jax.random.normal(own_key, extent, jnp.float32) * scale
    if len(cuts) > 0:
        array = block_scale(own_key, extent, cuts, -0.22, 0.18) * array
    return jnp.clip(array, min=-reach, max=reach).astype(kind)


def setup_inputs(seed: int = 0, part: int = 0) -> dict:
    key_of = jax.random.split(jax.random.key(seed), 7)
    part_keys = jax.random.split(jax.random.fold_in(key_of[6], part), 7)
    tokens = draw_tokens(jax.random.fold_in(jax.random.fold_in(key_of[6], part), 71), part)
    norm_gain = jnp.clip(1.0 + 0.1 * jax.random.normal(key_of[1], (D,), jnp.float32), 0.5, 1.5)
    router = noise(key_of[2], (D, EXPERTS), D ** -0.5, 0.09375)
    expert_ids_keys = jax.random.split(jax.random.fold_in(part_keys[3], 1), TOKENS // TOK_DEV)
    expert_ids_turns = jax.random.permutation(jax.random.fold_in(part_keys[3], 3), TOKENS // TOK_DEV)
    expert_ids = jax.vmap(lambda own, number: deal_out(jax.random.fold_in(part_keys[3], 2), own, number, TOK_DEV, EXPERTS, 2, CAP, 2))(expert_ids_keys, expert_ids_turns).reshape((TOKENS, 2))
    w_gate = noise(key_of[4], (N_EXPERT, LOCAL, D, FF_IDX), D ** -0.5, 0.09375, ((0, 4), (3, 4)))
    w_down = noise(key_of[5], (N_EXPERT, LOCAL, FF_IDX, D), FF ** -0.5, 0.0625, ((0, 4), (3, 4)))
    return dict(tokens=tokens, norm_gain=norm_gain, router=router, expert_ids=expert_ids, w_gate=w_gate, w_down=w_down)


epsilon = 1e-05

def expert_slots(expert_ids, experts, capacity):
    flat_ids = expert_ids.reshape(-1)
    onehot = (flat_ids[:, None] == jnp.arange(experts, dtype=jnp.int32)[None, :]).astype(jnp.int32)
    before = jnp.cumsum(onehot, axis=0) - onehot
    slot_index = lax.optimization_barrier(jnp.sum(before * onehot, axis=1)).astype(jnp.int32)
    return (flat_ids * capacity + slot_index).reshape(expert_ids.shape)

def gate_pair(logits, expert_ids):
    labels = jnp.arange(logits.shape[1], dtype=jnp.int32)
    picked = (expert_ids[:, :, None] == labels[None, None, :]).astype(jnp.float32)
    chosen = lax.optimization_barrier(jnp.sum(picked * logits[:, None, :], axis=2))
    first_gate = 1.0 / (1.0 + jnp.exp(chosen[:, 1] - chosen[:, 0]))
    second_gate = 1.0 / (1.0 + jnp.exp(chosen[:, 0] - chosen[:, 1]))
    return jnp.stack([first_gate, second_gate], axis=1).astype(jnp.bfloat16)

def one_expert(operands):
    row_block, gate_matrix, down_matrix = operands
    hidden = jax.nn.silu(jnp.dot(row_block, gate_matrix, preferred_element_type=jnp.float32)).astype(jnp.bfloat16)
    hidden = hidden.reshape(row_block.shape[0], PIECES, FF_IDX)
    piece_sums = jnp.einsum('rpf,pfd->rpd', hidden.astype(jnp.float32), down_matrix.astype(jnp.float32), precision=lax.Precision.HIGHEST).astype(jnp.bfloat16)
    piece_sums = lax.optimization_barrier(piece_sums)
    return lax.optimization_barrier(jnp.sum(piece_sums.astype(jnp.float32), axis=1))

def reference(tokens, norm_gain, router, expert_ids, w_gate, w_down):
    values = tokens.astype(jnp.float32)
    inverse_rms = lax.rsqrt(lax.optimization_barrier(jnp.mean(values * values, axis=1, keepdims=True)) + epsilon)
    normed = (values * inverse_rms * norm_gain[None, :]).astype(jnp.bfloat16)
    logits = jnp.dot(normed, router, preferred_element_type=jnp.float32)
    gate_values = gate_pair(logits, expert_ids)
    blocks = expert_ids.reshape(N_EXPERT, TOK_DEV, 2)
    slot_place = jax.vmap(partial(expert_slots, experts=EXPERTS, capacity=CAP))(blocks)
    slot_index = slot_place - blocks * CAP
    source = jnp.arange(N_EXPERT, dtype=jnp.int32)[:, None, None]
    row_index = (source * CAP + slot_index).reshape(-1).astype(jnp.int32)
    flat_ids = expert_ids.reshape(-1).astype(jnp.int32)
    repeated = jnp.repeat(normed, 2, axis=0)
    buffer = jnp.zeros((EXPERTS, N_EXPERT * CAP, D), jnp.bfloat16).at[flat_ids, row_index].set(repeated)
    gate_full = w_gate.reshape(EXPERTS // LOCAL, PIECES, LOCAL, D, FF_IDX).transpose(0, 2, 3, 1, 4).reshape(EXPERTS, D, FF)
    down_full = w_down.reshape(EXPERTS // LOCAL, PIECES, LOCAL, FF_IDX, D).transpose(0, 2, 1, 3, 4).reshape(EXPERTS, PIECES, FF_IDX, D)
    expert_out = lax.map(one_expert, (buffer, gate_full, down_full))
    gathered = expert_out[flat_ids, row_index].reshape(TOKENS, 2, D)
    mixed = lax.optimization_barrier(jnp.sum(gate_values.astype(jnp.float32)[:, :, None] * gathered, axis=1))
    return mixed.astype(jnp.bfloat16)
```

```python
import functools

import jax
import jax.numpy as jnp
from jax import lax
from jax.experimental import pallas as pl
from jax.experimental.pallas import tpu as pltpu
from jax.sharding import PartitionSpec as P

CAP = 40
epsilon = 1e-05
MESH = pl.DeviceIdType.MESH
F32 = jnp.float32
BF16 = jnp.bfloat16
NT = (((1,), (1,)), ((), ()))
TN = (((0,), (0,)), ((), ()))


def column_width(width):
    return 256 if width % 256 == 0 else width


def kernel(
    cfg, tok_ref, ids_ref, mix_ref, gain_ref, wg_hbm, wd_hbm, out_ref,
    wg, wd, send_rows, recv, xn, hid, acc, outb, ret, stat, comb, total,
    wg_sem, wd_sem, st_s, st_r, dz_s, dz_r, gx_s, gx_r, gp_s, gp_r,
    hx_s, hx_r, hp_s, hp_r, rz_s, rz_r,
):
    E, T, L, experts, pieces, slots = cfg
    X = T // 2
    e = lax.axis_index("expert")
    t = lax.axis_index("tensor")
    x, c = t // 2, lax.rem(t, 2)
    partner = x * 2 + 1 - c
    W = tok_ref.shape[1]
    rows_t = tok_ref.shape[0]
    NJ, D, cw = wg.shape[1:]
    FW = NJ * cw
    N = acc.shape[1]
    R = E * CAP

    def order(i):
        return lax.rem(e // 2 + i // 2, E // 2) * 2 + lax.rem(e + i, 2)

    def xpeer(k):
        return lax.rem(x + k, X)

    def gate_copy(l, j):
        cols = pl.ds(pl.multiple_of(j * cw, 128), cw) if NJ > 1 else pl.ds(0, cw)
        return pltpu.make_async_copy(wg_hbm.at[0, l, :, cols], wg.at[l, j], wg_sem.at[l, j])

    def peer(i):
        return lax.rem(x + i // 2, X) * 2 + lax.rem(c + i, 2)

    def down_copy(n):
        l, i = n // T, n % T
        rows = pl.ds(pl.multiple_of(peer(i) * FW, 16), FW)
        return pltpu.make_async_copy(wd_hbm.at[0, l, rows, :], wd.at[n % slots], wd_sem.at[n % slots])

    def remote(src, dst, ss, rs, **where):
        return pltpu.make_async_remote_copy(
            src_ref=src, dst_ref=dst, send_sem=ss, recv_sem=rs, device_id=where, device_id_type=MESH
        )

    barrier = pltpu.get_barrier_semaphore()
    for k in range(1, T):
        pl.semaphore_signal(barrier, inc=1, device_id={"tensor": lax.rem(t + k, T)}, device_id_type=MESH)
    for k in range(1, E):
        pl.semaphore_signal(barrier, inc=1, device_id={"expert": lax.rem(e + k, E)}, device_id_type=MESH)

    for l in range(L):
        for j in range(NJ):
            gate_copy(l, j).start()
    for n in range(min(slots, L * T)):
        down_copy(n).start()

    ids0, ids1 = ids_ref[0:1, :], ids_ref[1:2, :]
    label = lax.broadcasted_iota(jnp.int32, (experts, rows_t), 0)
    hot0 = (label == ids0).astype(F32)
    hot1 = (label == ids1).astype(F32)
    earlier = lax.broadcasted_iota(jnp.int32, (rows_t, rows_t), 0) < lax.broadcasted_iota(
        jnp.int32, (rows_t, rows_t), 1
    )
    before = jnp.dot(
        (hot0 + hot1).astype(BF16), earlier.astype(F32).astype(BF16), preferred_element_type=F32
    )
    slot0 = jnp.sum(hot0 * before, axis=0, keepdims=True)
    slot1 = jnp.sum(hot1 * (before + hot0), axis=0, keepdims=True)
    place0 = ids0 * CAP + slot0.astype(jnp.int32)
    place1 = ids1 * CAP + slot1.astype(jnp.int32)

    tokens = tok_ref[...]
    LC = L * CAP
    near = lax.broadcasted_iota(jnp.int32, (LC, rows_t), 0)
    for d in range(E):
        base = near + (d // pieces) * LC
        pick = jnp.where((base == place0) | (base == place1), 1.0, 0.0).astype(BF16)
        send_rows[d] = jnp.dot(pick, tokens, preferred_element_type=F32).astype(BF16)

    pl.semaphore_wait(barrier, T - 1 + E - 1)

    def dz(dest, src):
        return remote(send_rows.at[dest], recv.at[src, t], dz_s.at[dest], dz_r.at[src], expert=dest)

    for i in range(1, E):
        dz(order(i), e).start()
    recv[e, t] = send_rows[e]

    mix = mix_ref[...]
    mix_hi = mix.astype(BF16)
    mix_lo = (mix - mix_hi.astype(F32)).astype(BF16)
    logit = lax.dot_general(mix_hi, tokens, NT, preferred_element_type=F32)
    logit += lax.dot_general(mix_lo, tokens, NT, preferred_element_type=F32)
    sq = tokens.astype(F32) * tokens.astype(F32)
    sq_hi = sq.astype(BF16)
    sq_lo = (sq - sq_hi.astype(F32)).astype(BF16)
    ones = jnp.ones((8, W), BF16)
    squares = lax.dot_general(ones, sq_hi, NT, preferred_element_type=F32)
    squares += lax.dot_general(ones, sq_lo, NT, preferred_element_type=F32)
    stat[t, 0:experts, :] = logit
    stat[t, experts:, :] = squares

    def st(dest, src):
        return remote(stat.at[src], stat.at[src], st_s.at[dest], st_r.at[src], tensor=dest)

    for k in range(1, T):
        st(lax.rem(t + k, T), t).start()

    def gx(s, k):
        to = xpeer(k) * 2 + c
        return remote(recv.at[s, t], recv.at[s, t], gx_s.at[s, xpeer(k)], gx_r.at[s, x], tensor=to)

    def gx_in(s, k):
        q = xpeer(k) * 2 + c
        return remote(recv.at[s, q], recv.at[s, q], gx_s.at[s, xpeer(k)], gx_r.at[s, xpeer(k)], tensor=q)

    def gp(s, k):
        q = xpeer(k) * 2 + c
        return remote(
            recv.at[s, q], recv.at[s, q], gp_s.at[s, xpeer(k)], gp_r.at[s, xpeer(k)], tensor=partner
        )

    def gp_in(s, k):
        q = xpeer(k) * 2 + 1 - c
        return remote(
            recv.at[s, q], recv.at[s, q], gp_s.at[s, xpeer(k)], gp_r.at[s, xpeer(k)], tensor=partner
        )

    def spread(i):
        s = order(i)
        if i > 0:
            dz(s, s).wait_recv()
        for k in range(1, X):
            gx(s, k).start()
        gp(s, 0).start()

    def forward(i):
        s = order(i)
        for k in range(1, X):
            gx_in(s, k).wait_recv()
            gp(s, k).start()

    def arrived(i):
        s = order(i)
        for k in range(X):
            gp_in(s, k).wait_recv()

    def normalize(i):
        first = lax.rem(e // 2 + i // 2, E // 2)
        pair = (first * 2, first * 2 + 1)
        for s in pair:
            pass
        sums = []
        for s in pair:
            square = jnp.zeros((LC, 128), F32)
            for q in range(T):
                v = recv[s, q].astype(F32)
                v = v * v
                for b in range(W // 128):
                    square = square + v[:, b * 128:(b + 1) * 128]
            mean = jnp.sum(square, axis=1, keepdims=True) / D
            sums.append(lax.rsqrt(mean + epsilon))
        rows = pl.ds(pl.multiple_of(first * 2 * CAP, 16), 2 * CAP)
        for q in range(T):
            gain = gain_ref[:, q * W:(q + 1) * W]
            parts = [recv[s, q].astype(F32) * inv * gain for s, inv in zip(pair, sums)]
            for l in range(L):
                block = jnp.concatenate([p[l * CAP:(l + 1) * CAP] for p in parts], axis=0)
                xn[l, rows, q * W:(q + 1) * W] = block.astype(BF16)

    spread(0)

    for k in range(1, T):
        q = lax.rem(t + k, T)
        st(q, q).wait_recv()
    sums = stat[0]
    for q in range(1, T):
        sums = sums + stat[q]
    logits = sums[0:experts] * lax.rsqrt(sums[experts:] / D + epsilon)[0:1]
    chosen0 = jnp.sum(hot0 * logits, axis=0, keepdims=True)
    chosen1 = jnp.sum(hot1 * logits, axis=0, keepdims=True)
    gate0 = (1.0 / (1.0 + jnp.exp(chosen1 - chosen0))).astype(BF16).astype(F32)
    gate1 = (1.0 / (1.0 + jnp.exp(chosen0 - chosen1))).astype(BF16).astype(F32)
    slot_rows = lax.broadcasted_iota(jnp.int32, (CAP, rows_t), 0)
    for d in range(E):
        for l in range(L):
            base = slot_rows + ((d // pieces) * L + l) * CAP
            both = jnp.where(base == place0, gate0, 0.0) + jnp.where(base == place1, gate1, 0.0)
            comb[d, l] = both.astype(BF16)

    for i in range(1, E):
        spread(i)
        forward(i - 1)
        if i % 2 == 0:
            arrived(i - 2)
            arrived(i - 1)
            normalize(i - 2)
    forward(E - 1)
    arrived(E - 2)
    arrived(E - 1)
    normalize(E - 2)

    def hx(l, j, k):
        to = xpeer(k) * 2 + c
        return remote(
            hid.at[l, t, j], hid.at[l, t, j], hx_s.at[l, j, xpeer(k)], hx_r.at[l, j, x], tensor=to
        )

    def hx_in(l, j, k):
        q = xpeer(k) * 2 + c
        return remote(
            hid.at[l, q, j], hid.at[l, q, j], hx_s.at[l, j, xpeer(k)], hx_r.at[l, j, xpeer(k)], tensor=q
        )

    def hp(l, j, k):
        q = xpeer(k) * 2 + c
        return remote(
            hid.at[l, q, j], hid.at[l, q, j], hp_s.at[l, j, xpeer(k)], hp_r.at[l, j, xpeer(k)],
            tensor=partner,
        )

    def hp_in(l, j, k):
        q = xpeer(k) * 2 + 1 - c
        return remote(
            hid.at[l, q, j], hid.at[l, q, j], hp_s.at[l, j, xpeer(k)], hp_r.at[l, j, xpeer(k)],
            tensor=partner,
        )

    def pass_on(l, j):
        for k in range(1, X):
            hx_in(l, j, k).wait_recv()
            hp(l, j, k).start()

    for l in range(L):
        def gate_step(j, carry):
            gate_copy(l, j).wait()
            v = jnp.dot(xn[l], wg[l, j], preferred_element_type=F32)
            hid[l, t, j] = (v * (1.0 / (1.0 + jnp.exp(-v)))).astype(BF16)
            for k in range(1, X):
                hx(l, j, k).start()
            hp(l, j, 0).start()
            if l > 0:
                pass_on(l - 1, j)
            return carry

        lax.fori_loop(0, NJ, gate_step, 0)

    hosts = (L - 1) * T + 2
    passed = 0
    nw = 256 if N % 256 == 0 else N

    def rz(l, dest, src):
        return remote(outb.at[l, dest], ret.at[src, l], rz_s.at[l, dest], rz_r.at[l, src], expert=dest)

    for n in range(L * T):
        l, i = n // T, n % T
        q = peer(i)
        down_copy(n).wait()
        if i > 0:
            k = i // 2
            for j in range(NJ):
                if i % 2 == 1:
                    hp_in(l, j, k).wait_recv()
        slot = n % slots

        def down_step(b, carry):
            cols = pl.ds(pl.multiple_of(b * nw, 128), nw)
            lhs = jnp.concatenate([hid[l, q, j] for j in range(NJ)], axis=1) if NJ > 1 else hid[l, q, 0]
            v = jnp.dot(lhs, wd[slot, :, cols], preferred_element_type=F32)
            if i == 0:
                acc[:, cols] = v
            else:
                acc[:, cols] += v
            return carry

        lax.fori_loop(0, N // nw, down_step, 0)
        if n + slots < L * T:
            down_copy(n + slots).start()
        if n < hosts:
            until = (NJ * (n + 1)) // hosts
            for j in range(passed, until):
                pass_on(L - 1, j)
            passed = until
        if i == T - 1:
            for s in range(E):
                outb[l, s] = acc[s * CAP:(s + 1) * CAP, :].astype(BF16)
            for m in range(1, E):
                rz(l, order(m), e).start()
            ret[e, l] = outb[l, e]

    for l in range(L):
        for m in range(E):
            d = order(m)
            if m > 0:
                rz(l, d, d).wait_recv()
            v = lax.dot_general(comb[d, l], ret[d, l], TN, preferred_element_type=F32)
            if l == 0 and m == 0:
                total[...] = v
            else:
                total[...] += v
    out_ref[...] = total[...].astype(BF16)

    for k in range(1, T):
        st(lax.rem(t + k, T), t).wait_send()
    for i in range(1, E):
        dz(order(i), e).wait_send()
    for i in range(E):
        s = order(i)
        for k in range(1, X):
            gx(s, k).wait_send()
        for k in range(X):
            gp(s, k).wait_send()
    for l in range(L):
        for j in range(NJ):
            for k in range(1, X):
                hx(l, j, k).wait_send()
            for k in range(X):
                hp(l, j, k).wait_send()
        for m in range(1, E):
            rz(l, order(m), e).wait_send()


def on_device(tokens, norm_gain, router, expert_ids, w_gate, w_down):
    rows_t, W = tokens.shape
    experts = router.shape[1]
    E, T = lax.axis_size("expert"), lax.axis_size("tensor")
    L = w_gate.shape[1]
    pieces = max(1, E // experts)
    D = norm_gain.shape[0]
    FW = w_gate.shape[3]
    N = w_down.shape[3]
    cw = column_width(FW)
    NJ = FW // cw
    X = T // 2
    R = E * CAP
    slots = min(6, L * T)
    first = lax.axis_index("tensor") * W
    gain_part = lax.dynamic_slice_in_dim(norm_gain, first, W, 0)
    router_part = lax.dynamic_slice_in_dim(router, first, W, 0)
    mix = (router_part.astype(F32) * gain_part[:, None]).T
    DMA = pltpu.SemaphoreType.DMA
    vmem = pl.BlockSpec(memory_space=pltpu.VMEM)
    hbm = pl.BlockSpec(memory_space=pl.ANY)
    return pl.pallas_call(
        functools.partial(kernel, (E, T, L, experts, pieces, slots)),
        out_shape=jax.ShapeDtypeStruct((rows_t, N), BF16),
        in_specs=[vmem, vmem, vmem, vmem, hbm, hbm],
        out_specs=vmem,
        scratch_shapes=[
            pltpu.VMEM((L, NJ, D, cw), BF16),
            pltpu.VMEM((slots, FW, N), BF16),
            pltpu.VMEM((E, L * CAP, W), BF16),
            pltpu.VMEM((E, T, L * CAP, W), BF16),
            pltpu.VMEM((L, R, D), BF16),
            pltpu.VMEM((L, T, NJ, R, cw), BF16),
            pltpu.VMEM((R, N), F32),
            pltpu.VMEM((L, E, CAP, N), BF16),
            pltpu.VMEM((E, L, CAP, N), BF16),
            pltpu.VMEM((T, experts + 8, rows_t), F32),
            pltpu.VMEM((E, L, CAP, rows_t), BF16),
            pltpu.VMEM((rows_t, N), F32),
            DMA((L, NJ)), DMA((slots,)),
            DMA((T,)), DMA((T,)), DMA((E,)), DMA((E,)),
            DMA((E, X)), DMA((E, X)), DMA((E, X)), DMA((E, X)),
            DMA((L, NJ, X)), DMA((L, NJ, X)), DMA((L, NJ, X)), DMA((L, NJ, X)),
            DMA((L, E)), DMA((L, E)),
        ],
        compiler_params=pltpu.CompilerParams(
            collective_id=0, has_side_effects=True, vmem_limit_bytes=67043328
        ),
    )(tokens, expert_ids.T, mix, norm_gain[None, :], w_gate, w_down)


def solution(mesh):
    return jax.shard_map(
        on_device,
        mesh=mesh,
        in_specs=(
            P(("groups", "expert"), "tensor"),
            P(),
            P(),
            P(("groups", "expert"), None),
            P("expert", None, None, "tensor"),
            P("expert", None, None, "tensor"),
        ),
        out_specs=P(("groups", "expert"), "tensor"),
        check_vma=False,
    )
```

```python
import functools

import jax
import jax.numpy as jnp
from jax import lax
from jax.experimental import pallas as pl
from jax.experimental.pallas import tpu as pltpu
from jax.sharding import PartitionSpec as P

CAP = 40
epsilon = 1e-05
MESH = pl.DeviceIdType.MESH
F32 = jnp.float32
BF16 = jnp.bfloat16
NT = (((1,), (1,)), ((), ()))
TN = (((0,), (0,)), ((), ()))


def column_width(width):
    return 256 if width % 256 == 0 else width


def kernel(
    cfg, tok_ref, ids_ref, router_ref, gain_ref, wg_hbm, wd_hbm, out_ref,
    wg, wd, send_rows, recv, xn, hid, acc, outb, ret, stat, comb, total,
    wg_sem, wd_sem, st_s, st_r, dz_s, dz_r, gx_s, gx_r, gp_s, gp_r,
    hx_s, hx_r, hp_s, hp_r, rz_s, rz_r,
):
    E, T, L, experts, pieces, slots = cfg
    X = T // 2
    e = lax.axis_index("expert")
    t = lax.axis_index("tensor")
    x, c = t // 2, lax.rem(t, 2)
    partner = x * 2 + 1 - c
    W = tok_ref.shape[1]
    rows_t = tok_ref.shape[0]
    NJ, D, cw = wg.shape[1:]
    FW = NJ * cw
    N = acc.shape[1]
    R = E * CAP

    def order(i):
        return lax.rem(e // 2 + i // 2, E // 2) * 2 + lax.rem(e + i, 2)

    def xpeer(k):
        return lax.rem(x + k, X)

    def gate_copy(l, j):
        cols = pl.ds(pl.multiple_of(j * cw, 128), cw) if NJ > 1 else pl.ds(0, cw)
        return pltpu.make_async_copy(wg_hbm.at[0, l, :, cols], wg.at[l, j], wg_sem.at[l, j])

    def peer(i):
        return lax.rem(x + i // 2, X) * 2 + lax.rem(c + i, 2)

    def down_copy(n):
        l, i = n // T, n % T
        rows = pl.ds(pl.multiple_of(peer(i) * FW, 16), FW)
        return pltpu.make_async_copy(wd_hbm.at[0, l, rows, :], wd.at[n % slots], wd_sem.at[n % slots])

    def remote(src, dst, ss, rs, **where):
        return pltpu.make_async_remote_copy(
            src_ref=src, dst_ref=dst, send_sem=ss, recv_sem=rs, device_id=where, device_id_type=MESH
        )

    barrier = pltpu.get_barrier_semaphore()
    for k in range(1, T):
        pl.semaphore_signal(barrier, inc=1, device_id={"tensor": lax.rem(t + k, T)}, device_id_type=MESH)
    for k in range(1, E):
        pl.semaphore_signal(barrier, inc=1, device_id={"expert": lax.rem(e + k, E)}, device_id_type=MESH)

    for l in range(L):
        for j in range(NJ):
            gate_copy(l, j).start()
    for n in range(min(slots, L * T)):
        down_copy(n).start()

    ids0, ids1 = ids_ref[0:1, :], ids_ref[1:2, :]
    label = lax.broadcasted_iota(jnp.int32, (experts, rows_t), 0)
    hot0 = (label == ids0).astype(F32)
    hot1 = (label == ids1).astype(F32)
    earlier = lax.broadcasted_iota(jnp.int32, (rows_t, rows_t), 0) < lax.broadcasted_iota(
        jnp.int32, (rows_t, rows_t), 1
    )
    before = jnp.dot(
        (hot0 + hot1).astype(BF16), earlier.astype(F32).astype(BF16), preferred_element_type=F32
    )
    slot0 = jnp.sum(hot0 * before, axis=0, keepdims=True)
    slot1 = jnp.sum(hot1 * (before + hot0), axis=0, keepdims=True)
    place0 = ids0 * CAP + slot0.astype(jnp.int32)
    place1 = ids1 * CAP + slot1.astype(jnp.int32)

    tokens = tok_ref[...]
    LC = L * CAP
    near = lax.broadcasted_iota(jnp.int32, (LC, rows_t), 0)
    for d in range(E):
        base = near + (d // pieces) * LC
        pick = jnp.where((base == place0) | (base == place1), 1.0, 0.0).astype(BF16)
        send_rows[d] = jnp.dot(pick, tokens, preferred_element_type=F32).astype(BF16)

    pl.semaphore_wait(barrier, T - 1 + E - 1)

    def dz(dest, src):
        return remote(send_rows.at[dest], recv.at[src, t], dz_s.at[dest], dz_r.at[src], expert=dest)

    for i in range(1, E):
        dz(order(i), e).start()
    recv[e, t] = send_rows[e]

    own = pl.ds(pl.multiple_of(t * W, 128), W)
    mix = router_ref[:, own].astype(F32) * gain_ref[:, own]
    mix_hi = mix.astype(BF16)
    mix_lo = (mix - mix_hi.astype(F32)).astype(BF16)
    logit = lax.dot_general(mix_hi, tokens, NT, preferred_element_type=F32)
    logit += lax.dot_general(mix_lo, tokens, NT, preferred_element_type=F32)
    sq = tokens.astype(F32) * tokens.astype(F32)
    sq_hi = sq.astype(BF16)
    sq_lo = (sq - sq_hi.astype(F32)).astype(BF16)
    ones = jnp.ones((8, W), BF16)
    squares = lax.dot_general(ones, sq_hi, NT, preferred_element_type=F32)
    squares += lax.dot_general(ones, sq_lo, NT, preferred_element_type=F32)
    stat[t, 0:experts, :] = logit
    stat[t, experts:, :] = squares

    def st(dest, src):
        return remote(stat.at[src], stat.at[src], st_s.at[dest], st_r.at[src], tensor=dest)

    for k in range(1, T):
        st(lax.rem(t + k, T), t).start()

    def gx(s, k):
        to = xpeer(k) * 2 + c
        return remote(recv.at[s, t], recv.at[s, t], gx_s.at[s, xpeer(k)], gx_r.at[s, x], tensor=to)

    def gx_in(s, k):
        q = xpeer(k) * 2 + c
        return remote(recv.at[s, q], recv.at[s, q], gx_s.at[s, xpeer(k)], gx_r.at[s, xpeer(k)], tensor=q)

    def gp(s, k):
        q = xpeer(k) * 2 + c
        return remote(
            recv.at[s, q], recv.at[s, q], gp_s.at[s, xpeer(k)], gp_r.at[s, xpeer(k)], tensor=partner
        )

    def gp_in(s, k):
        q = xpeer(k) * 2 + 1 - c
        return remote(
            recv.at[s, q], recv.at[s, q], gp_s.at[s, xpeer(k)], gp_r.at[s, xpeer(k)], tensor=partner
        )

    def spread(i):
        s = order(i)
        if i > 0:
            dz(s, s).wait_recv()
        for k in range(1, X):
            gx(s, k).start()
        gp(s, 0).start()

    def forward(i):
        s = order(i)
        for k in range(1, X):
            gx_in(s, k).wait_recv()
            gp(s, k).start()

    def arrived(i):
        s = order(i)
        for k in range(X):
            gp_in(s, k).wait_recv()

    def normalize(i):
        first = lax.rem(e // 2 + i // 2, E // 2)
        pair = (first * 2, first * 2 + 1)
        sums = []
        for s in pair:
            square = jnp.zeros((LC, 128), F32)
            for q in range(T):
                v = recv[s, q].astype(F32)
                v = v * v
                for b in range(W // 128):
                    square = square + v[:, b * 128:(b + 1) * 128]
            mean = jnp.sum(square, axis=1, keepdims=True) / D
            sums.append(lax.rsqrt(mean + epsilon))
        rows = pl.ds(i * CAP, 2 * CAP)
        for q in range(T):
            gain = gain_ref[:, q * W:(q + 1) * W]
            parts = [recv[s, q].astype(F32) * inv * gain for s, inv in zip(pair, sums)]
            for l in range(L):
                block = jnp.concatenate([p[l * CAP:(l + 1) * CAP] for p in parts], axis=0)
                xn[l, rows, q * W:(q + 1) * W] = block.astype(BF16)

    spread(0)

    for k in range(1, T):
        q = lax.rem(t + k, T)
        st(q, q).wait_recv()
    sums = stat[0]
    for q in range(1, T):
        sums = sums + stat[q]
    logits = sums[0:experts] * lax.rsqrt(sums[experts:] / D + epsilon)[0:1]
    chosen0 = jnp.sum(hot0 * logits, axis=0, keepdims=True)
    chosen1 = jnp.sum(hot1 * logits, axis=0, keepdims=True)
    gate0 = (1.0 / (1.0 + jnp.exp(chosen1 - chosen0))).astype(BF16).astype(F32)
    gate1 = (1.0 / (1.0 + jnp.exp(chosen0 - chosen1))).astype(BF16).astype(F32)
    slot_rows = lax.broadcasted_iota(jnp.int32, (CAP, rows_t), 0)
    for d in range(E):
        for l in range(L):
            base = slot_rows + ((d // pieces) * L + l) * CAP
            both = jnp.where(base == place0, gate0, 0.0) + jnp.where(base == place1, gate1, 0.0)
            comb[d, l] = both.astype(BF16)

    half_rows = (pl.ds(0, 2 * CAP), pl.ds(2 * CAP, R - 2 * CAP))

    def hid_copy(l, h, j, k, mine, sems, to):
        block = hid.at[l, xpeer(k) * 2 + (c if mine else 1 - c), j, half_rows[h]]
        return remote(
            block, block, sems[0].at[l, j, xpeer(k), h], sems[1].at[l, j, xpeer(k), h], tensor=to
        )

    def hx(l, h, j, k):
        block = hid.at[l, t, j, half_rows[h]]
        return remote(
            block, block, hx_s.at[l, j, xpeer(k), h], hx_r.at[l, j, x, h], tensor=xpeer(k) * 2 + c
        )

    def hx_in(l, h, j, k):
        return hid_copy(l, h, j, k, True, (hx_s, hx_r), xpeer(k) * 2 + c)

    def hp(l, h, j, k):
        return hid_copy(l, h, j, k, True, (hp_s, hp_r), partner)

    def hp_in(l, h, j, k):
        return hid_copy(l, h, j, k, False, (hp_s, hp_r), partner)

    def send_hidden(l, h, j):
        for k in range(1, X):
            hx(l, h, j, k).start()
        hp(l, h, j, 0).start()

    def pass_on(l, h, j):
        for k in range(1, X):
            hx_in(l, h, j, k).wait_recv()
            hp(l, h, j, k).start()

    def silu(v):
        return (v * (1.0 / (1.0 + jnp.exp(-v)))).astype(BF16)

    def near_step(j, carry):
        gate_copy(0, j).wait()
        rows = half_rows[0]
        hid[0, t, j, rows] = silu(jnp.dot(xn[0, rows], wg[0, j], preferred_element_type=F32))
        send_hidden(0, 0, j)
        return carry

    def far_step(j, carry):
        rows = half_rows[1]
        hid[0, t, j, rows] = silu(jnp.dot(xn[0, rows], wg[0, j], preferred_element_type=F32))
        send_hidden(0, 1, j)
        pass_on(0, 0, j)
        return carry

    spread(1)
    forward(0)
    forward(1)
    spread(2)
    arrived(0)
    arrived(1)
    normalize(0)
    early = min(3, NJ)
    lax.fori_loop(0, early, near_step, 0)
    for i in range(3, E):
        spread(i)
        forward(i - 1)
    lax.fori_loop(early, NJ, near_step, 0)
    forward(E - 1)
    for i in range(2, E, 2):
        arrived(i)
        arrived(i + 1)
        normalize(i)
    lax.fori_loop(0, NJ, far_step, 0)

    for l in range(1, L):
        def gate_step(j, carry):
            gate_copy(l, j).wait()
            hid[l, t, j] = silu(jnp.dot(xn[l], wg[l, j], preferred_element_type=F32))
            send_hidden(l, 1, j)
            pass_on(l - 1, 1, j)
            if l > 1:
                pass_on(l - 1, 0, j)
            return carry

        lax.fori_loop(0, NJ, gate_step, 0)

        def near_send(j, carry):
            send_hidden(l, 0, j)
            return carry

        lax.fori_loop(0, NJ, near_send, 0)

    pending = [(L - 1, 1, j) for j in range(NJ)]
    if L > 1:
        pending += [(L - 1, 0, j) for j in range(NJ)]

    def drain(count):
        for _ in range(min(count, len(pending))):
            pass_on(*pending.pop(0))

    nw = 256 if N % 256 == 0 else N

    def rz(l, dest, src):
        return remote(outb.at[l, dest], ret.at[src, l], rz_s.at[l, dest], rz_r.at[l, src], expert=dest)

    groups = [(l, (0, 1)) for l in range(L - 1)] + [(L - 1, (1,)), (L - 1, (0,))]
    for l, halves in groups:
        rows = half_rows[halves[0]] if len(halves) == 1 else pl.ds(0, R)
        for i in range(T):
            n, q = l * T + i, peer(i)
            slot = n % slots
            if halves != (0,):
                down_copy(n).wait()
            if i > 0:
                while any(u[0] == l and u[1] in halves for u in pending) and i > 1:
                    drain(1)
                if i % 2 == 1:
                    for h in halves:
                        for j in range(NJ):
                            hp_in(l, h, j, i // 2).wait_recv()

            def down_step(b, carry):
                cols = pl.ds(pl.multiple_of(b * nw, 128), nw)
                lhs = [hid[l, q, j, rows] for j in range(NJ)]
                lhs = jnp.concatenate(lhs, axis=1) if NJ > 1 else lhs[0]
                v = jnp.dot(lhs, wd[slot, :, cols], preferred_element_type=F32)
                if i == 0:
                    acc[rows, cols] = v
                else:
                    acc[rows, cols] += v
                return carry

            lax.fori_loop(0, N // nw, down_step, 0)
            if len(halves) == 2 and n + slots < L * T:
                down_copy(n + slots).start()
            if halves != (0,):
                drain(NJ * (i + 1) // T - NJ * i // T)
        out_of = [m for h in halves for m in (range(2) if h == 0 else range(2, E))]
        for m in out_of:
            s = lax.rem(e // 2 + m // 2, E // 2) * 2 + m % 2
            outb[l, s] = acc[m * CAP:(m + 1) * CAP, :].astype(BF16)
        for m in out_of:
            if m > 0:
                rz(l, order(m), e).start()
            else:
                ret[e, l] = outb[l, e]

    returns = [(l, m) for l in range(L - 1) for m in range(E)]
    returns += [(L - 1, m) for m in list(range(2, E)) + [0, 1]]
    for l, m in returns:
        d = order(m)
        if m > 0:
            rz(l, d, d).wait_recv()
        v = lax.dot_general(comb[d, l], ret[d, l], TN, preferred_element_type=F32)
        if (l, m) == returns[0]:
            total[...] = v
        else:
            total[...] += v
    out_ref[...] = total[...]

    for k in range(1, T):
        st(lax.rem(t + k, T), t).wait_send()
    for i in range(1, E):
        dz(order(i), e).wait_send()
    for i in range(E):
        s = order(i)
        for k in range(1, X):
            gx(s, k).wait_send()
        for k in range(X):
            gp(s, k).wait_send()
    for l in range(L):
        for j in range(NJ):
            for h in range(2):
                for k in range(1, X):
                    hx(l, h, j, k).wait_send()
                for k in range(X):
                    hp(l, h, j, k).wait_send()
        for m in range(1, E):
            rz(l, order(m), e).wait_send()


def on_device(tokens, norm_gain, router, expert_ids, w_gate, w_down):
    rows_t, W = tokens.shape
    experts = router.shape[1]
    E, T = lax.axis_size("expert"), lax.axis_size("tensor")
    L = w_gate.shape[1]
    pieces = max(1, E // experts)
    D = norm_gain.shape[0]
    FW = w_gate.shape[3]
    N = w_down.shape[3]
    cw = column_width(FW)
    NJ = FW // cw
    X = T // 2
    R = E * CAP
    slots = min(T + 2, L * T)
    DMA = pltpu.SemaphoreType.DMA
    vmem = pl.BlockSpec(memory_space=pltpu.VMEM)
    hbm = pl.BlockSpec(memory_space=pl.ANY)
    return pl.pallas_call(
        functools.partial(kernel, (E, T, L, experts, pieces, slots)),
        out_shape=jax.ShapeDtypeStruct((rows_t, N), F32),
        in_specs=[vmem, vmem, vmem, vmem, hbm, hbm],
        out_specs=vmem,
        scratch_shapes=[
            pltpu.VMEM((L, NJ, D, cw), BF16),
            pltpu.VMEM((slots, FW, N), BF16),
            pltpu.VMEM((E, L * CAP, W), BF16),
            pltpu.VMEM((E, T, L * CAP, W), BF16),
            pltpu.VMEM((L, R, D), BF16),
            pltpu.VMEM((L, T, NJ, R, cw), BF16),
            pltpu.VMEM((R, N), F32),
            pltpu.VMEM((L, E, CAP, N), BF16),
            pltpu.VMEM((E, L, CAP, N), BF16),
            pltpu.VMEM((T, experts + 8, rows_t), F32),
            pltpu.VMEM((E, L, CAP, rows_t), BF16),
            pltpu.VMEM((rows_t, N), F32),
            DMA((L, NJ)), DMA((slots,)),
            DMA((T,)), DMA((T,)), DMA((E,)), DMA((E,)),
            DMA((E, X)), DMA((E, X)), DMA((E, X)), DMA((E, X)),
            DMA((L, NJ, X, 2)), DMA((L, NJ, X, 2)), DMA((L, NJ, X, 2)), DMA((L, NJ, X, 2)),
            DMA((L, E)), DMA((L, E)),
        ],
        compiler_params=pltpu.CompilerParams(
            collective_id=0, has_side_effects=True, vmem_limit_bytes=67043328
        ),
    )(tokens, expert_ids.T, router.T, norm_gain[None, :], w_gate, w_down).astype(BF16)


def solution(mesh):
    return jax.shard_map(
        on_device,
        mesh=mesh,
        in_specs=(
            P(("groups", "expert"), "tensor"),
            P(),
            P(),
            P(("groups", "expert"), None),
            P("expert", None, None, "tensor"),
            P("expert", None, None, "tensor"),
        ),
        out_specs=P(("groups", "expert"), "tensor"),
        check_vma=False,
    )
```

```python
import functools

import jax
import jax.numpy as jnp
from jax import lax
from jax.experimental import pallas as pl
from jax.experimental.pallas import tpu as pltpu
from jax.sharding import PartitionSpec as P

CAP = 40
epsilon = 1e-05
MESH = pl.DeviceIdType.MESH
F32 = jnp.float32
BF16 = jnp.bfloat16
NT = (((1,), (1,)), ((), ()))
TN = (((0,), (0,)), ((), ()))


def column_width(width):
    return 256 if width % 256 == 0 else width


def kernel(
    cfg, tok_ref, ids_ref, router_ref, gain_ref, wg_hbm, wd_hbm, out_ref,
    wg, wd, send_rows, recv, xn, hid, acc, outb, ret, stat, comb, total,
    wg_sem, wd_sem, st_s, st_r, dz_s, dz_r, gx_s, gx_r, gp_s, gp_r,
    hx_s, hx_r, hp_s, hp_r, rz_s, rz_r,
):
    E, T, L, experts, pieces, slots = cfg
    X = T // 2
    e = lax.axis_index("expert")
    t = lax.axis_index("tensor")
    x, c = t // 2, lax.rem(t, 2)
    partner = x * 2 + 1 - c
    W = tok_ref.shape[1]
    rows_t = tok_ref.shape[0]
    NJ, D, cw = wg.shape[1:]
    FW = NJ * cw
    N = acc.shape[1]
    R = E * CAP

    def order(i):
        return lax.rem(e // 2 + i // 2, E // 2) * 2 + lax.rem(e + i, 2)

    def xpeer(k):
        return lax.rem(x + k, X)

    def gate_copy(l, j):
        cols = pl.ds(pl.multiple_of(j * cw, 128), cw) if NJ > 1 else pl.ds(0, cw)
        return pltpu.make_async_copy(wg_hbm.at[0, l, :, cols], wg.at[l, j], wg_sem.at[l, j])

    def peer(i):
        return lax.rem(x + i // 2, X) * 2 + lax.rem(c + i, 2)

    def down_copy(n):
        l, i = n // T, n % T
        rows = pl.ds(pl.multiple_of(peer(i) * FW, 16), FW)
        return pltpu.make_async_copy(wd_hbm.at[0, l, rows, :], wd.at[n % slots], wd_sem.at[n % slots])

    def remote(src, dst, ss, rs, **where):
        return pltpu.make_async_remote_copy(
            src_ref=src, dst_ref=dst, send_sem=ss, recv_sem=rs, device_id=where, device_id_type=MESH
        )

    barrier = pltpu.get_barrier_semaphore()
    for k in range(1, T):
        pl.semaphore_signal(barrier, inc=1, device_id={"tensor": lax.rem(t + k, T)}, device_id_type=MESH)
    for k in range(1, E):
        pl.semaphore_signal(barrier, inc=1, device_id={"expert": lax.rem(e + k, E)}, device_id_type=MESH)

    for l in range(L):
        for j in range(NJ):
            gate_copy(l, j).start()
    for n in range(min(slots, L * T)):
        down_copy(n).start()

    ids0, ids1 = ids_ref[0:1, :], ids_ref[1:2, :]
    label = lax.broadcasted_iota(jnp.int32, (experts, rows_t), 0)
    hot0 = (label == ids0).astype(F32)
    hot1 = (label == ids1).astype(F32)
    earlier = lax.broadcasted_iota(jnp.int32, (rows_t, rows_t), 0) < lax.broadcasted_iota(
        jnp.int32, (rows_t, rows_t), 1
    )
    before = jnp.dot(
        (hot0 + hot1).astype(BF16), earlier.astype(F32).astype(BF16), preferred_element_type=F32
    )
    slot0 = jnp.sum(hot0 * before, axis=0, keepdims=True)
    slot1 = jnp.sum(hot1 * (before + hot0), axis=0, keepdims=True)
    place0 = ids0 * CAP + slot0.astype(jnp.int32)
    place1 = ids1 * CAP + slot1.astype(jnp.int32)

    tokens = tok_ref[...]
    LC = L * CAP
    near = lax.broadcasted_iota(jnp.int32, (LC, rows_t), 0)
    for d in range(E):
        base = near + (d // pieces) * LC
        pick = jnp.where((base == place0) | (base == place1), 1.0, 0.0).astype(BF16)
        send_rows[d] = jnp.dot(pick, tokens, preferred_element_type=F32).astype(BF16)

    pl.semaphore_wait(barrier, T - 1 + E - 1)

    def dz(dest, src):
        return remote(send_rows.at[dest], recv.at[src, t], dz_s.at[dest], dz_r.at[src], expert=dest)

    for i in range(1, E):
        dz(order(i), e).start()
    recv[e, t] = send_rows[e]

    own = pl.ds(pl.multiple_of(t * W, 128), W)
    mix = router_ref[:, own].astype(F32) * gain_ref[:, own]
    mix_hi = mix.astype(BF16)
    mix_lo = (mix - mix_hi.astype(F32)).astype(BF16)
    logit = lax.dot_general(mix_hi, tokens, NT, preferred_element_type=F32)
    logit += lax.dot_general(mix_lo, tokens, NT, preferred_element_type=F32)
    sq = tokens.astype(F32) * tokens.astype(F32)
    sq_hi = sq.astype(BF16)
    sq_lo = (sq - sq_hi.astype(F32)).astype(BF16)
    ones = jnp.ones((8, W), BF16)
    squares = lax.dot_general(ones, sq_hi, NT, preferred_element_type=F32)
    squares += lax.dot_general(ones, sq_lo, NT, preferred_element_type=F32)
    stat[t, 0:experts, :] = logit
    stat[t, experts:, :] = squares

    def st(dest, src):
        return remote(stat.at[src], stat.at[src], st_s.at[dest], st_r.at[src], tensor=dest)

    for k in range(1, T):
        st(lax.rem(t + k, T), t).start()

    def gx(s, k):
        to = xpeer(k) * 2 + c
        return remote(recv.at[s, t], recv.at[s, t], gx_s.at[s, xpeer(k)], gx_r.at[s, x], tensor=to)

    def gx_in(s, k):
        q = xpeer(k) * 2 + c
        return remote(recv.at[s, q], recv.at[s, q], gx_s.at[s, xpeer(k)], gx_r.at[s, xpeer(k)], tensor=q)

    def gp(s, k):
        q = xpeer(k) * 2 + c
        return remote(
            recv.at[s, q], recv.at[s, q], gp_s.at[s, xpeer(k)], gp_r.at[s, xpeer(k)], tensor=partner
        )

    def gp_in(s, k):
        q = xpeer(k) * 2 + 1 - c
        return remote(
            recv.at[s, q], recv.at[s, q], gp_s.at[s, xpeer(k)], gp_r.at[s, xpeer(k)], tensor=partner
        )

    def spread(i):
        s = order(i)
        if i > 0:
            dz(s, s).wait_recv()
        for k in range(1, X):
            gx(s, k).start()
        gp(s, 0).start()

    def forward(i):
        s = order(i)
        for k in range(1, X):
            gx_in(s, k).wait_recv()
            gp(s, k).start()

    def arrived(i):
        s = order(i)
        for k in range(X):
            gp_in(s, k).wait_recv()

    def normalize(i):
        first = lax.rem(e // 2 + i // 2, E // 2)
        pair = (first * 2, first * 2 + 1)
        sums = []
        for s in pair:
            square = jnp.zeros((LC, 128), F32)
            for q in range(T):
                v = recv[s, q].astype(F32)
                v = v * v
                for b in range(W // 128):
                    square = square + v[:, b * 128:(b + 1) * 128]
            mean = jnp.sum(square, axis=1, keepdims=True) / D
            sums.append(lax.rsqrt(mean + epsilon))
        rows = pl.ds(i * CAP, 2 * CAP)
        for q in range(T):
            gain = gain_ref[:, q * W:(q + 1) * W]
            parts = [recv[s, q].astype(F32) * inv * gain for s, inv in zip(pair, sums)]
            for l in range(L):
                block = jnp.concatenate([p[l * CAP:(l + 1) * CAP] for p in parts], axis=0)
                xn[l, rows, q * W:(q + 1) * W] = block.astype(BF16)

    spread(0)

    for k in range(1, T):
        q = lax.rem(t + k, T)
        st(q, q).wait_recv()
    sums = stat[0]
    for q in range(1, T):
        sums = sums + stat[q]
    logits = sums[0:experts] * lax.rsqrt(sums[experts:] / D + epsilon)[0:1]
    chosen0 = jnp.sum(hot0 * logits, axis=0, keepdims=True)
    chosen1 = jnp.sum(hot1 * logits, axis=0, keepdims=True)
    gate0 = (1.0 / (1.0 + jnp.exp(chosen1 - chosen0))).astype(BF16).astype(F32)
    gate1 = (1.0 / (1.0 + jnp.exp(chosen0 - chosen1))).astype(BF16).astype(F32)
    slot_rows = lax.broadcasted_iota(jnp.int32, (CAP, rows_t), 0)
    for d in range(E):
        for l in range(L):
            base = slot_rows + ((d // pieces) * L + l) * CAP
            both = jnp.where(base == place0, gate0, 0.0) + jnp.where(base == place1, gate1, 0.0)
            comb[d, l] = both.astype(BF16)

    half_rows = (pl.ds(0, 2 * CAP), pl.ds(2 * CAP, R - 2 * CAP))

    def hid_copy(l, h, j, k, mine, sems, to):
        block = hid.at[l, xpeer(k) * 2 + (c if mine else 1 - c), j, half_rows[h]]
        return remote(
            block, block, sems[0].at[l, j, xpeer(k), h], sems[1].at[l, j, xpeer(k), h], tensor=to
        )

    def hx(l, h, j, k):
        block = hid.at[l, t, j, half_rows[h]]
        return remote(
            block, block, hx_s.at[l, j, xpeer(k), h], hx_r.at[l, j, x, h], tensor=xpeer(k) * 2 + c
        )

    def hx_in(l, h, j, k):
        return hid_copy(l, h, j, k, True, (hx_s, hx_r), xpeer(k) * 2 + c)

    def hp(l, h, j, k):
        return hid_copy(l, h, j, k, True, (hp_s, hp_r), partner)

    def hp_in(l, h, j, k):
        return hid_copy(l, h, j, k, False, (hp_s, hp_r), partner)

    def send_hidden(l, h, j):
        for k in range(1, X):
            hx(l, h, j, k).start()
        hp(l, h, j, 0).start()

    def pass_on(l, h, j):
        for k in range(1, X):
            hx_in(l, h, j, k).wait_recv()
            hp(l, h, j, k).start()

    def silu(v):
        return (v * (1.0 / (1.0 + jnp.exp(-v)))).astype(BF16)

    def near_step(j, carry):
        gate_copy(0, j).wait()
        rows = half_rows[0]
        hid[0, t, j, rows] = silu(jnp.dot(xn[0, rows], wg[0, j], preferred_element_type=F32))
        send_hidden(0, 0, j)
        return carry

    def far_step(j, carry):
        rows = half_rows[1]
        hid[0, t, j, rows] = silu(jnp.dot(xn[0, rows], wg[0, j], preferred_element_type=F32))
        send_hidden(0, 1, j)
        pass_on(0, 0, j)
        return carry

    spread(1)
    forward(0)
    forward(1)
    spread(2)
    arrived(0)
    arrived(1)
    normalize(0)
    early = min(3, NJ)
    lax.fori_loop(0, early, near_step, 0)
    for i in range(3, E):
        spread(i)
        forward(i - 1)
    lax.fori_loop(early, NJ, near_step, 0)
    forward(E - 1)
    for i in range(2, E, 2):
        arrived(i)
        arrived(i + 1)
        normalize(i)
    lax.fori_loop(0, NJ, far_step, 0)

    for l in range(1, L):
        def gate_step(j, carry):
            gate_copy(l, j).wait()
            hid[l, t, j] = silu(jnp.dot(xn[l], wg[l, j], preferred_element_type=F32))
            send_hidden(l, 1, j)
            pass_on(l - 1, 1, j)
            if l > 1:
                pass_on(l - 1, 0, j)
            return carry

        lax.fori_loop(0, NJ, gate_step, 0)

        def near_send(j, carry):
            send_hidden(l, 0, j)
            return carry

        lax.fori_loop(0, NJ, near_send, 0)

    pending = [(L - 1, 1, j) for j in range(NJ)]
    if L > 1:
        pending += [(L - 1, 0, j) for j in range(NJ)]

    def drain(count):
        for _ in range(min(count, len(pending))):
            pass_on(*pending.pop(0))

    nw = 512 if N % 512 == 0 else N

    def rz(l, dest, src):
        return remote(outb.at[l, dest], ret.at[src, l], rz_s.at[l, dest], rz_r.at[l, src], expert=dest)

    groups = [(l, (0, 1)) for l in range(L - 1)] + [(L - 1, (1,)), (L - 1, (0,))]
    for l, halves in groups:
        rows = half_rows[halves[0]] if len(halves) == 1 else pl.ds(0, R)
        for i in range(T):
            n, q = l * T + i, peer(i)
            slot = n % slots
            if halves != (0,):
                down_copy(n).wait()
            if i > 0:
                while any(u[0] == l and u[1] in halves for u in pending) and i > 1:
                    drain(1)
                if i % 2 == 1:
                    for h in halves:
                        for j in range(NJ):
                            hp_in(l, h, j, i // 2).wait_recv()

            def down_step(b, carry):
                cols = pl.ds(pl.multiple_of(b * nw, 128), nw)
                lhs = [hid[l, q, j, rows] for j in range(NJ)]
                lhs = jnp.concatenate(lhs, axis=1) if NJ > 1 else lhs[0]
                v = jnp.dot(lhs, wd[slot, :, cols], preferred_element_type=F32)
                if i == 0:
                    acc[rows, cols] = v
                else:
                    acc[rows, cols] += v
                return carry

            lax.fori_loop(0, N // nw, down_step, 0)
            if len(halves) == 2 and n + slots < L * T:
                down_copy(n + slots).start()
            if halves != (0,):
                drain(NJ * (i + 1) // T - NJ * i // T)
        out_of = [m for h in halves for m in (range(2) if h == 0 else range(2, E))]
        for m in out_of:
            s = lax.rem(e // 2 + m // 2, E // 2) * 2 + m % 2
            outb[l, s] = acc[m * CAP:(m + 1) * CAP, :].astype(BF16)
        for m in out_of:
            if m > 0:
                rz(l, order(m), e).start()
            else:
                ret[e, l] = outb[l, e]

    returns = [(l, m) for l in range(L - 1) for m in range(E)]
    returns += [(L - 1, m) for m in list(range(2, E)) + [0, 1]]
    for l, m in returns:
        d = order(m)
        if m > 0:
            rz(l, d, d).wait_recv()
        v = lax.dot_general(comb[d, l], ret[d, l], TN, preferred_element_type=F32)
        if (l, m) == returns[0]:
            total[...] = v
        else:
            total[...] += v
    out_ref[...] = total[...]

    for k in range(1, T):
        st(lax.rem(t + k, T), t).wait_send()
    for i in range(1, E):
        dz(order(i), e).wait_send()
    for i in range(E):
        s = order(i)
        for k in range(1, X):
            gx(s, k).wait_send()
        for k in range(X):
            gp(s, k).wait_send()
    for l in range(L):
        for j in range(NJ):
            for h in range(2):
                for k in range(1, X):
                    hx(l, h, j, k).wait_send()
                for k in range(X):
                    hp(l, h, j, k).wait_send()
        for m in range(1, E):
            rz(l, order(m), e).wait_send()


def on_device(tokens, norm_gain, router, expert_ids, w_gate, w_down):
    rows_t, W = tokens.shape
    experts = router.shape[1]
    E, T = lax.axis_size("expert"), lax.axis_size("tensor")
    L = w_gate.shape[1]
    pieces = max(1, E // experts)
    D = norm_gain.shape[0]
    FW = w_gate.shape[3]
    N = w_down.shape[3]
    cw = column_width(FW)
    NJ = FW // cw
    X = T // 2
    R = E * CAP
    slots = min(T + 2, L * T)
    DMA = pltpu.SemaphoreType.DMA
    vmem = pl.BlockSpec(memory_space=pltpu.VMEM)
    hbm = pl.BlockSpec(memory_space=pl.ANY)
    return pl.pallas_call(
        functools.partial(kernel, (E, T, L, experts, pieces, slots)),
        out_shape=jax.ShapeDtypeStruct((rows_t, N), F32),
        in_specs=[vmem, vmem, vmem, vmem, hbm, hbm],
        out_specs=vmem,
        scratch_shapes=[
            pltpu.VMEM((L, NJ, D, cw), BF16),
            pltpu.VMEM((slots, FW, N), BF16),
            pltpu.VMEM((E, L * CAP, W), BF16),
            pltpu.VMEM((E, T, L * CAP, W), BF16),
            pltpu.VMEM((L, R, D), BF16),
            pltpu.VMEM((L, T, NJ, R, cw), BF16),
            pltpu.VMEM((R, N), F32),
            pltpu.VMEM((L, E, CAP, N), BF16),
            pltpu.VMEM((E, L, CAP, N), BF16),
            pltpu.VMEM((T, experts + 8, rows_t), F32),
            pltpu.VMEM((E, L, CAP, rows_t), BF16),
            pltpu.VMEM((rows_t, N), F32),
            DMA((L, NJ)), DMA((slots,)),
            DMA((T,)), DMA((T,)), DMA((E,)), DMA((E,)),
            DMA((E, X)), DMA((E, X)), DMA((E, X)), DMA((E, X)),
            DMA((L, NJ, X, 2)), DMA((L, NJ, X, 2)), DMA((L, NJ, X, 2)), DMA((L, NJ, X, 2)),
            DMA((L, E)), DMA((L, E)),
        ],
        compiler_params=pltpu.CompilerParams(
            collective_id=0, has_side_effects=True, vmem_limit_bytes=67043328
        ),
    )(tokens, expert_ids.T, router.T, norm_gain[None, :], w_gate, w_down).astype(BF16)


def solution(mesh):
    return jax.shard_map(
        on_device,
        mesh=mesh,
        in_specs=(
            P(("groups", "expert"), "tensor"),
            P(),
            P(),
            P(("groups", "expert"), None),
            P("expert", None, None, "tensor"),
            P("expert", None, None, "tensor"),
        ),
        out_specs=P(("groups", "expert"), "tensor"),
        check_vma=False,
    )
```
